32 devices in a mesh: stream: 4 (over y, core), azim: 8 (over z, x).
Axes of the slice: x: 2, y: 2, z: 4, core: 2. Of those that a mesh axis runs over, the one named last changes fastest.
Arguments:
- fluid: float32 [4, 256, 256, 128], P(None, 'stream', 'azim'), may hold values from -4 to 4
- bubbles: float32 [16384, 5, 128], P(('stream', 'azim'))
- counts: int32 [32], P(('stream', 'azim')), may hold values from 128 to 512
- outgoing_block_order: int32 [16384], P(('stream', 'azim')), may hold values from 0 to 511, as said below
- tiles_first_update: int32 [16384], P(('stream', 'azim')), may hold values from 0 to 2047
- tiles_after: int32 [16384], P(('stream', 'azim')), may hold values from 0 to 2047
Outputs:
- fluid_out: float32 [4, 256, 256, 128], P(None, 'stream', 'azim')
- bubbles_out: float32 [16384, 5, 128], P(('stream', 'azim'))
- void_fraction: float32 [256, 256, 128], P('stream', 'azim')
The draws below stay inside these ranges and needn't reach their ends.
Inputs may be any that keep to these rules, and one draw needn't show every extreme that they name: `outgoing_block_order`: for each device, its 512 entries are each of 0 to 511 once.
All inputs are finite; a program needn't handle non-finite values.
Results may differ from the reference program's by a relative error of at most 0.000076.
Values sent between devices are 32-bit elements; how exact they have to be, the bound alone decides.
A program may use at most 128 MiB of HBM per device.

```python
import math
import jax
import jax.numpy as jnp
import numpy as np
from jax import lax

CS = 64
CA = 32
CR = 128
BB = 128
NBLK = 512
SUBSTEPS = 8
NTILE = 2048
CAP = 16
NS = 256
NAZ = 256
NBT = 16384
N_AZIM = 8
DEVICES = 32


def draw_bubbles(key, part):
    uniform_draw = jax.random.uniform(key, (NBT, 5, BB), jnp.float32)
    lower = jnp.array([0.8, -0.3, 4.0, -1.0, 0.8], jnp.float32)
    upper = jnp.array([1.25, 0.3, CR - 5.0, 1.0, 1.2], jnp.float32)
    return (lower[None, :, None] + (upper - lower)[None, :, None] * uniform_draw).astype(jnp.float32)


def draw_outgoing_block_order(key, part):
    device_keys = jax.random.split(jax.random.fold_in(key, 17), NBT // NBLK)
    orders = jax.vmap(lambda single: jax.random.permutation(single, NBLK))(device_keys)
    return orders.reshape(-1).astype(jnp.int32)


def plant(values, key, least, top_value):
    longest = values.shape.index(max(values.shape))
    spots = []
    for shift in (0, 1):
        where = [jax.random.randint(jax.random.fold_in(key, axis), (), 0, length) for axis, length in enumerate(values.shape)]
        where[longest] = (where[longest] + shift) % values.shape[longest]
        spots.append(tuple(where))
    return values.at[spots[0]].set(least).at[spots[1]].set(top_value)


def steps_of(key, shape, shards, low, largest):
    def one(dim, blocks):
        steps = jax.random.uniform(jax.random.fold_in(jax.random.fold_in(key, 6), dim), (blocks,), jnp.float32, low / len(shards), largest / len(shards))
        return jnp.repeat(jnp.exp(steps), shape[dim] // blocks).reshape((-1,) + (1,) * (len(shape) - dim - 1))

    loudness = one(*shards[0])
    for cut in shards[1:]:
        loudness = loudness * one(*cut)
    return loudness


def rank_bounds(amount, slope):
    weights = [(1 << 20) // math.isqrt(standing ** slope) + 1 for standing in range(1, amount + 1)]
    deviation = 1 + sum(weights) // (1 << 30)
    return np.cumsum(np.array([max(1, weight // deviation) for weight in weights]))


def skewed_ids(own_key, extent, amount, lean):
    table = rank_bounds(amount, lean)
    ticket = jax.random.randint(jax.random.fold_in(own_key, 1), extent, 0, int(table[amount - 1]))
    grade = jnp.searchsorted(jnp.asarray(table, jnp.int32), ticket, side="right")
    return jax.random.permutation(jax.random.fold_in(own_key, 2), amount)[grade].astype(jnp.int32)


def bell_draw(own_key, dims, deviation, bound, shards=(), kind=jnp.bfloat16):
    gain = steps_of(own_key, dims, shards, -0.22, 0.18) if shards else 1.0
    values = jax.random.normal(own_key, dims, jnp.float32) * deviation * gain
    return jnp.minimum(jnp.maximum(values, -bound), bound).astype(kind)


def setup_inputs(seed: int = 0) -> dict:
    key_of = jax.random.split(jax.random.key(seed), 7)
    fluid = bell_draw(key_of[0], (4, NS, NAZ, CR), 1.0, 4.0, ((1, 4), (2, 8)), jnp.float32)
    bubbles = draw_bubbles(jax.random.fold_in(key_of[6], 71), 0)
    counts = plant(jax.random.randint(key_of[2], (DEVICES,), NBLK // 4, NBLK + 1), jax.random.fold_in(key_of[2], 1), NBLK // 4, NBLK).astype(jnp.int32)
    outgoing_block_order = draw_outgoing_block_order(jax.random.fold_in(key_of[6], 71), 0)
    tiles_first_update = plant(skewed_ids(key_of[4], (NBT,), NTILE, 1), jax.random.fold_in(key_of[4], 3), 0, NTILE - 1).astype(jnp.int32)
    tiles_after = plant(skewed_ids(key_of[5], (NBT,), NTILE, 1), jax.random.fold_in(key_of[5], 3), 0, NTILE - 1).astype(jnp.int32)
    return {"fluid": fluid, "bubbles": bubbles, "counts": counts, "outgoing_block_order": outgoing_block_order, "tiles_first_update": tiles_first_update, "tiles_after": tiles_after}


TIME_STEP = 0.25
MEAN_FLOW = 0.5
DIFFUSION = 0.1
KERNEL_WIDTH = 1.5
GAS_INDEX = 4.2
PRESSURE_COUPLING = 0.3
AMBIENT = 1.0
RELAX_TIME = 0.5
VISCOUS = 0.08
SOURCE_GAIN = 0.05
VOID_SCALE = 0.01
FOUR_PI = 12.566370614359172


def kernel_weights(position, cell_centres):
    offset = (position[:, :, None] - cell_centres) / KERNEL_WIDTH
    raw = jnp.exp(-0.5 * offset * offset)
    return raw / jnp.sum(raw, axis=-1, keepdims=True)


def advance_group(packed_blocks):
    bubble_state, tile_row_count, alive_flags = packed_blocks
    cell_centres = jnp.arange(tile_row_count.shape[-1], dtype=jnp.int32).astype(jnp.float32)
    weights = kernel_weights(bubble_state[:, 2], cell_centres)
    sampled = jnp.einsum("gbk,gck->gcb", weights, tile_row_count, precision=lax.Precision.HIGHEST)
    pressure = sampled[:, 0]
    velocity = sampled[:, 1]
    radius = bubble_state[:, 0]
    growth = bubble_state[:, 1]
    position = bubble_state[:, 2]
    bubble_speed = bubble_state[:, 3]
    rest_radius = bubble_state[:, 4]
    substep_size = TIME_STEP / SUBSTEPS
    for substep in range(SUBSTEPS):
        gas = jnp.exp(GAS_INDEX * jnp.log(rest_radius / radius))
        accel = (gas - AMBIENT - PRESSURE_COUPLING * pressure - 1.5 * growth * growth - VISCOUS * growth / radius) / radius
        growth = growth + substep_size * accel
        radius = radius + substep_size * growth
        bubble_speed = bubble_speed + substep_size * (velocity - bubble_speed) / RELAX_TIME
        position = position + substep_size * bubble_speed
    new_state = jnp.stack([radius, growth, position, bubble_speed, rest_radius], axis=1)
    weights = kernel_weights(position, cell_centres)
    source_amounts = jnp.stack([SOURCE_GAIN * FOUR_PI * radius * radius * growth,
                         VOID_SCALE * FOUR_PI / 3.0 * radius * radius * radius], axis=1)
    source_amounts = source_amounts * alive_flags[:, None, None]
    spread_sources = jnp.einsum("gbk,gcb->gck", weights, source_amounts, precision=lax.Precision.HIGHEST)
    return new_state, spread_sources


def advance_every_group(bubble_state, tile_row_count, alive_flags):
    bubble_groups = bubble_state.shape[0] // 64
    new_state, spread_sources = lax.map(advance_group, (bubble_state.reshape((bubble_groups, 64) + bubble_state.shape[1:]),
                                                tile_row_count.reshape((bubble_groups, 64) + tile_row_count.shape[1:]),
                                                alive_flags.reshape(bubble_groups, 64)))
    return new_state.reshape(bubble_state.shape), spread_sources.reshape(tile_row_count.shape)


def fluid_update(flow_field, stream_up, stream_down, azim_up, azim_down, radial_up, radial_down, source):
    d_stream = 0.5 * (stream_up - stream_down)
    d_azim = 0.5 * (azim_up - azim_down)
    d_radial = 0.5 * (radial_up - radial_down)
    pressure_rate = -MEAN_FLOW * d_stream[0] - d_stream[1] - d_azim[2] - d_radial[3] - source
    stream_rate = -MEAN_FLOW * d_stream[1] - d_stream[0]
    azim_rate = -MEAN_FLOW * d_stream[2] - d_azim[0]
    radial_rate = -MEAN_FLOW * d_stream[3] - d_radial[0]
    change = jnp.stack([pressure_rate, stream_rate, azim_rate, radial_rate])
    laplace = stream_up + stream_down + azim_up + azim_down + radial_up + radial_down - 6.0 * flow_field
    return flow_field + TIME_STEP * change + DIFFUSION * laplace


def fluid_step(flow_field, source):
    padded = jnp.pad(flow_field, ((0, 0), (1, 1), (0, 0), (1, 1)))
    return fluid_update(flow_field, padded[:, 2:, :, 1:-1], padded[:, :-2, :, 1:-1],
                        jnp.roll(flow_field, -1, axis=2), jnp.roll(flow_field, 1, axis=2),
                        padded[:, 1:-1, :, 2:], padded[:, 1:-1, :, :-2], source)


def global_update(flow_field, bubble_state, tile_indices, alive_flags):
    slot_index = jnp.arange(NBT, dtype=jnp.int32)
    owner_device = slot_index // NBLK
    stream_cell = (owner_device // N_AZIM) * CS + tile_indices // CA
    azim_cell = (owner_device % N_AZIM) * CA + tile_indices % CA
    selected = jnp.stack([flow_field[0], flow_field[3]])
    tile_row_count = selected[:, stream_cell, azim_cell].transpose(1, 0, 2)
    bubble_state, spread_sources = advance_every_group(bubble_state, tile_row_count, alive_flags)
    grid = jnp.zeros((2,) + flow_field.shape[1:], jnp.float32).at[:, stream_cell, azim_cell].add(spread_sources.transpose(1, 0, 2))
    return fluid_step(flow_field, grid[0]), bubble_state, grid[1]


def reference(fluid, bubbles, counts, outgoing_block_order, tiles_first_update, tiles_after):
    slot_index = jnp.arange(NBT, dtype=jnp.int32)
    owner_device = slot_index // NBLK
    local_slot_index = slot_index % NBLK
    alive_flags = (local_slot_index < counts[owner_device]).astype(jnp.float32)
    flow_field, bubble_state, void_before_update = global_update(fluid, bubbles, tiles_first_update, alive_flags)
    source_device = local_slot_index // CAP
    within = local_slot_index % CAP
    position_sent = source_device * NBLK + owner_device * CAP + within
    sender_slot_index = (source_device * NBLK + outgoing_block_order[position_sent]).astype(jnp.int32)
    moved = bubble_state[sender_slot_index]
    moved_alive_flags = alive_flags[sender_slot_index]
    flow_field, bubble_state, void_field = global_update(flow_field, moved, tiles_after, moved_alive_flags)
    return flow_field, bubble_state * moved_alive_flags[:, None, None], void_field
```

```python
import functools

import jax
import jax.numpy as jnp
from jax import lax
from jax.experimental import pallas as pl
from jax.experimental.pallas import tpu as pltpu
from jax.sharding import PartitionSpec as P

SUBSTEPS = 8
TIME_STEP = 0.25
MEAN_FLOW = 0.5
DIFFUSION = 0.1
KERNEL_WIDTH = 1.5
GAS_INDEX = 4.2
PRESSURE_COUPLING = 0.3
AMBIENT = 1.0
RELAX_TIME = 0.5
VISCOUS = 0.08
SOURCE_GAIN = 0.05
VOID_SCALE = 0.01
FOUR_PI = 12.566370614359172
GROUP = 8
STATES = 5
ROWS = GROUP * STATES
WIDE = 4


def split_bf16(values):
    high = values.astype(jnp.bfloat16)
    low = (values - high.astype(jnp.float32)).astype(jnp.bfloat16)
    return high, low


def stacked_lhs(rows):
    high = rows.astype(jnp.bfloat16).astype(jnp.float32)
    both = jnp.concatenate([high, rows - high], axis=0).astype(jnp.bfloat16)
    return jnp.concatenate([both, both], axis=1)


def raw_weights(position_row, cells):
    offset = cells - position_row
    return jnp.exp(offset * offset * (-0.5 / (KERNEL_WIDTH * KERNEL_WIDTH)))


def bubble_kernel(first, *refs):
    if first:
        (order_ref, tiles_ref, count_ref, bubbles_ref, p_ref, u_ref,
         state_ref, source_ref, sp, su, sn, amounts, rows) = refs
        void_ref = None
        old_ref = state_ref
    else:
        (tiles_ref, old_ref, p_ref, u_ref,
         bubbles_out, source_ref, void_ref, sp, su, sn, amounts, rows, state_ref) = refs
    cells_n, lanes = p_ref.shape[1:][-1], sp.shape[1]
    groups = sp.shape[0] // GROUP
    cells = lax.broadcasted_iota(jnp.int32, (cells_n, lanes), 0).astype(jnp.float32)
    source_ref[...] = jnp.zeros_like(source_ref)
    if void_ref is not None:
        void_ref[...] = jnp.zeros_like(void_ref)
    rows[...] = jnp.zeros_like(rows)
    amounts[...] = jnp.zeros_like(amounts)
    for pair in range(GROUP // 2):
        rows[8 * pair + 2 : 8 * pair + 3, :] = jnp.ones((1, cells_n), jnp.float32)

    if first:
        state_row = lax.broadcasted_iota(jnp.int32, (STATES, lanes), 0)
        marker = jnp.where(state_row == 0, -1.0, 1.0)

    def tile_of(slot):
        return tiles_ref[order_ref[slot]] if first else tiles_ref[slot]

    def sample(g, carry):
        base = g * GROUP
        for j in range(GROUP):
            tile = tile_of(base + j)
            if first:
                block = order_ref[base + j]
                block_state = jnp.where(block < count_ref[0], bubbles_ref[block], marker)
                state_ref[pl.ds(g * ROWS + j, STATES, stride=GROUP), :] = block_state
            at = 4 * j
            rows[at : at + 1, :] = p_ref[0, pl.ds(tile, 1), :]
            rows[at + 1 : at + 2, :] = u_ref[0, pl.ds(tile, 1), :]
        for pair in range(GROUP // 2):
            highs, lows = [], []
            for j in (2 * pair, 2 * pair + 1):
                position = old_ref[pl.ds(g * ROWS + 2 * GROUP + j, 1), :]
                high, low = split_bf16(raw_weights(position, cells))
                highs.append(high)
                lows.append(low)
            rhs = jnp.concatenate(
                [jnp.concatenate(highs, axis=1), jnp.concatenate(lows, axis=1)], axis=0
            )
            lhs = stacked_lhs(rows[8 * pair : 8 * pair + 8, :])
            result = jnp.dot(lhs, rhs, preferred_element_type=jnp.float32)
            result = result[:8] + result[8:]
            for side in range(2):
                part = result[:, side * lanes : (side + 1) * lanes]
                at = base + 2 * pair + side
                sp[pl.ds(at, 1), :] = part[4 * side : 4 * side + 1]
                su[pl.ds(at, 1), :] = part[4 * side + 1 : 4 * side + 2]
                sn[pl.ds(at, 1), :] = part[2:3]
        return carry

    lax.fori_loop(0, groups, sample, 0)

    def advance(w, carry):
        for i in range(WIDE):
            g = w * WIDE + i
            row = pl.multiple_of(g * GROUP, GROUP)
            at = [pl.multiple_of(g * ROWS + c * GROUP, GROUP) for c in range(STATES)]
            radius, growth, position, speed, rest = (
                old_ref[pl.ds(a, GROUP), :] for a in at
            )
            live = radius * rest >= 0.0
            radius = jnp.where(live, radius, 1.0)
            inverse = 1.0 / sn[pl.ds(row, GROUP), :]
            pressure = sp[pl.ds(row, GROUP), :] * inverse
            velocity = su[pl.ds(row, GROUP), :] * inverse
            drive = AMBIENT + PRESSURE_COUPLING * pressure
            h = TIME_STEP / SUBSTEPS
            for _ in range(SUBSTEPS):
                over = 1.0 / radius
                gas = jnp.exp(GAS_INDEX * jnp.log(rest * over))
                accel = (gas - drive - 1.5 * growth * growth - VISCOUS * growth * over) * over
                growth = growth + h * accel
                radius = radius + h * growth
                speed = speed + (h / RELAX_TIME) * (velocity - speed)
                position = position + h * speed
            source = SOURCE_GAIN * FOUR_PI * radius * radius * growth
            amounts[pl.ds(g * 4 * GROUP, GROUP, stride=4), :] = jnp.where(live, source, 0.0)
            if first:
                radius = jnp.where(live, radius, -1.0)
                new = (radius, growth, position, speed, rest)
            else:
                void = VOID_SCALE * FOUR_PI / 3.0 * radius * radius * radius
                amounts[pl.ds(g * 4 * GROUP + 1, GROUP, stride=4), :] = jnp.where(live, void, 0.0)
                new = tuple(
                    jnp.where(live, x, 0.0) for x in (radius, growth, position, speed, rest)
                )
            for a, x in zip(at, new):
                state_ref[pl.ds(a, GROUP), :] = x
        return carry

    lax.fori_loop(0, groups // WIDE, advance, 0)

    def spread(g, carry):
        base = g * GROUP
        sublane = lax.broadcasted_iota(jnp.int32, (8, lanes), 0)
        for pair in range(GROUP // 2):
            pieces, norms = [], []
            for j in (2 * pair, 2 * pair + 1):
                position = state_ref[pl.ds(g * ROWS + 2 * GROUP + j, 1), :]
                raw = raw_weights(position, cells)
                norms.append(jnp.sum(raw, axis=0, keepdims=True))
                pieces.append(jnp.concatenate(split_bf16(raw), axis=1))
            rhs = jnp.concatenate(pieces, axis=0)
            amount = amounts[pl.ds(pl.multiple_of(g * 4 * GROUP + 8 * pair, 8), 8), :]
            amount = amount / jnp.where(sublane < 4, norms[0], norms[1])
            result = lax.dot_general(
                stacked_lhs(amount), rhs, (((1,), (1,)), ((), ())),
                preferred_element_type=jnp.float32,
            )
            result = result[:8] + result[8:]
            for side in range(2):
                part = result[:, side * cells_n : (side + 1) * cells_n]
                slot = base + 2 * pair + side
                tile = tile_of(slot)
                source_ref[pl.ds(tile, 1), :] += part[4 * side : 4 * side + 1]
                if void_ref is not None:
                    void_ref[pl.ds(tile, 1), :] += part[4 * side + 1 : 4 * side + 2]
                    bubbles_out[slot] = state_ref[
                        pl.ds(g * ROWS + 2 * pair + side, STATES, stride=GROUP), :
                    ]
        return carry

    lax.fori_loop(0, groups, spread, 0)


def bubble_step(first, fluid, scalars, state):
    comps, tiles, cells = fluid.shape
    lanes = state.shape[-1]
    slots = scalars[0].shape[0]
    field = jax.ShapeDtypeStruct((tiles, cells), jnp.float32)
    packed = (slots * STATES, lanes)
    scratch = [pltpu.VMEM((slots, lanes), jnp.float32) for _ in range(3)]
    scratch += [pltpu.VMEM((4 * slots, lanes), jnp.float32), pltpu.VMEM((32, cells), jnp.float32)]
    if first:
        outs = (jax.ShapeDtypeStruct(packed, jnp.float32), field)
    else:
        outs = (jax.ShapeDtypeStruct((slots, STATES, lanes), jnp.float32), field, field)
        scratch.append(pltpu.VMEM(packed, jnp.float32))
    whole = lambda shape: pl.BlockSpec(shape, lambda i: (0,) * len(shape))
    work = slots * lanes * cells
    return pl.pallas_call(
        functools.partial(bubble_kernel, first),
        grid=(1,),
        out_shape=outs,
        in_specs=[pl.BlockSpec(memory_space=pltpu.SMEM)] * len(scalars)
        + [
            whole(state.shape),
            pl.BlockSpec((1, tiles, cells), lambda i: (0, 0, 0)),
            pl.BlockSpec((1, tiles, cells), lambda i: (3, 0, 0)),
        ],
        out_specs=tuple(whole(o.shape) for o in outs),
        scratch_shapes=scratch,
        compiler_params=pltpu.CompilerParams(vmem_limit_bytes=40 * 2**20),
        cost_estimate=pl.CostEstimate(
            flops=work * 40, bytes_accessed=12 * 2**20, transcendentals=2 * work
        ),
        name="bubbles_first" if first else "bubbles_second",
    )(*scalars, state, fluid, fluid)


def fluid_kernel(edges, f_ref, before_ref, after_ref, low_ref, high_ref, left_ref, right_ref,
                 source_ref, out_ref, *edge_refs):
    step, steps = pl.program_id(0), pl.num_programs(0)
    comps, depth, width, cells = f_ref.shape
    row = lax.broadcasted_iota(jnp.int32, (width, cells), 0)
    lane = lax.broadcasted_iota(jnp.int32, (width, cells), 1)
    at_start, at_end = step == 0, step == steps - 1
    for s in range(depth):
        now, below, above = [], [], []
        for c in range(comps):
            now.append(f_ref[c, s])
            below.append(
                jnp.where(at_start, low_ref[c, 0], before_ref[c, 0]) if s == 0 else f_ref[c, s - 1]
            )
            above.append(
                jnp.where(at_end, high_ref[c, 0], after_ref[c, 0])
                if s == depth - 1
                else f_ref[c, s + 1]
            )
        d_s, d_a, d_r, lap = [], [], [], []
        for c in range(comps):
            x = now[c]
            a_down = jnp.where(row == 0, left_ref[c, s : s + 1, :], pltpu.roll(x, 1, 0))
            a_up = jnp.where(
                row == width - 1, right_ref[c, s : s + 1, :], pltpu.roll(x, width - 1, 0)
            )
            r_down = jnp.where(lane == 0, 0.0, pltpu.roll(x, 1, 1))
            r_up = jnp.where(lane == cells - 1, 0.0, pltpu.roll(x, cells - 1, 1))
            d_s.append(above[c] - below[c])
            d_a.append(a_up - a_down)
            d_r.append(r_up - r_down)
            lap.append(above[c] + below[c] + a_up + a_down + r_up + r_down - 6.0 * x)
        half = 0.5 * TIME_STEP
        change = [
            MEAN_FLOW * d_s[0] + d_s[1] + d_a[2] + d_r[3],
            MEAN_FLOW * d_s[1] + d_s[0],
            MEAN_FLOW * d_s[2] + d_a[0],
            MEAN_FLOW * d_s[3] + d_r[0],
        ]
        for c in range(comps):
            new = now[c] - half * change[c] + DIFFUSION * lap[c]
            if c == 0:
                new = new - TIME_STEP * source_ref[s]
            out_ref[c, s] = new
            if edges:
                edge_refs[0][c, s : s + 1, :] = new[0:1]
                edge_refs[1][c, s : s + 1, :] = new[width - 1 : width]


def fluid_step(edges, fluid, halos, source):
    comps, length, width, cells = fluid.shape
    depth = 8
    steps = length // depth
    plane = (comps, 1, width, cells)
    side = pl.BlockSpec((comps, depth, cells), lambda i: (0, i, 0))
    still = pl.BlockSpec(plane, lambda i: (0, 0, 0, 0))
    main = pl.BlockSpec((comps, depth, width, cells), lambda i: (0, i, 0, 0))
    outs = [jax.ShapeDtypeStruct(fluid.shape, jnp.float32)]
    out_specs = [main]
    if edges:
        outs += [jax.ShapeDtypeStruct((comps, length, cells), jnp.float32)] * 2
        out_specs += [side, side]
    return pl.pallas_call(
        functools.partial(fluid_kernel, edges),
        grid=(steps,),
        out_shape=tuple(outs),
        in_specs=[
            main,
            pl.BlockSpec(plane, lambda i: (0, jnp.maximum(i * depth - 1, 0), 0, 0)),
            pl.BlockSpec(plane, lambda i: (0, jnp.minimum(i * depth + depth, length - 1), 0, 0)),
            still,
            still,
            side,
            side,
            pl.BlockSpec((depth, width, cells), lambda i: (i, 0, 0)),
        ],
        out_specs=tuple(out_specs),
        compiler_params=pltpu.CompilerParams(vmem_limit_bytes=24 * 2**20),
        cost_estimate=pl.CostEstimate(
            flops=fluid.size * 30, bytes_accessed=10 * 2**20, transcendentals=0
        ),
        name="fluid_first" if edges else "fluid_second",
    )(fluid, fluid, fluid, *halos, source)


def exchange(fluid, first_col, last_col):
    streams, azims = lax.axis_size("stream"), lax.axis_size("azim")
    length = fluid.shape[1]
    up = [(i, i + 1) for i in range(streams - 1)]
    down = [(i + 1, i) for i in range(streams - 1)]
    right = [(i, (i + 1) % azims) for i in range(azims)]
    left = [((i + 1) % azims, i) for i in range(azims)]
    return (
        lax.ppermute(fluid[:, length - 1 :], "stream", up),
        lax.ppermute(fluid[:, :1], "stream", down),
        lax.ppermute(last_col, "azim", right),
        lax.ppermute(first_col, "azim", left),
    )


def on_device(fluid, bubbles, counts, outgoing_block_order, tiles_first_update, tiles_after):
    comps, length, width, cells = fluid.shape
    slots, states, lanes = bubbles.shape
    devices = lax.axis_size("stream") * lax.axis_size("azim")
    cap = slots // devices
    flat = (comps, length * width, cells)
    grid = (length, width, cells)
    halos = exchange(fluid, fluid[:, :, 0], fluid[:, :, width - 1])
    sent, source = bubble_step(
        True, fluid.reshape(flat), (outgoing_block_order, tiles_first_update, counts), bubbles
    )
    axes = ("stream", "azim")
    if cap % GROUP == 0:
        sent = sent.reshape(devices, cap * states, lanes)
        arrived = lax.all_to_all(sent, axes, split_axis=0, concat_axis=0, tiled=True)
    else:
        sent = sent.reshape(slots // GROUP, states, GROUP, lanes).transpose(0, 2, 1, 3)
        sent = sent.reshape(devices, cap * states, lanes)
        arrived = lax.all_to_all(sent, axes, split_axis=0, concat_axis=0, tiled=True)
        arrived = arrived.reshape(slots // GROUP, GROUP, states, lanes).transpose(0, 2, 1, 3)
    arrived = arrived.reshape(slots * states, lanes)
    fluid, first_col, last_col = fluid_step(True, fluid, halos, source.reshape(grid))
    halos = exchange(fluid, first_col, last_col)
    bubbles, source, void = bubble_step(False, fluid.reshape(flat), (tiles_after,), arrived)
    (fluid,) = fluid_step(False, fluid, halos, source.reshape(grid))
    return fluid, bubbles, void.reshape(grid)


def solution(mesh):
    return jax.shard_map(
        on_device,
        mesh=mesh,
        in_specs=(
            P(None, "stream", "azim", None),
            P(("stream", "azim"), None, None),
            P(("stream", "azim")),
            P(("stream", "azim")),
            P(("stream", "azim")),
            P(("stream", "azim")),
        ),
        out_specs=(
            P(None, "stream", "azim", None),
            P(("stream", "azim"), None, None),
            P("stream", "azim", None),
        ),
        check_vma=False,
    )
```

```python
import functools

import jax
import jax.numpy as jnp
from jax import lax
from jax.experimental import pallas as pl
from jax.experimental.pallas import tpu as pltpu
from jax.sharding import PartitionSpec as P


SUBSTEPS = 8
TIME_STEP = 0.25
MEAN_FLOW = 0.5
DIFFUSION = 0.1
KERNEL_WIDTH = 1.5
GAS_INDEX = 4.2
PRESSURE_COUPLING = 0.3
AMBIENT = 1.0
RELAX_TIME = 0.5
VISCOUS = 0.08
SOURCE_GAIN = 0.05
VOID_SCALE = 0.01
FOUR_PI = 12.566370614359172
LOG2E = 1.4426950408889634
GROUP = 8
STATES = 5
ROWS = GROUP * STATES
WIDE = 4
UNROLL = 2


def split_bf16(values):
    high = values.astype(jnp.bfloat16)
    low = (values - high.astype(jnp.float32)).astype(jnp.bfloat16)
    return high, low


def stacked_lhs(rows):
    high = rows.astype(jnp.bfloat16).astype(jnp.float32)
    both = jnp.concatenate([high, rows - high], axis=0).astype(jnp.bfloat16)
    return jnp.concatenate([both, both], axis=1)


def raw_weights(position_row, cells):
    offset = cells - position_row
    return jnp.exp2(offset * offset * (-0.5 * LOG2E / (KERNEL_WIDTH * KERNEL_WIDTH)))


def cell_centres(cells_n, lanes):
    return lax.broadcasted_iota(jnp.int32, (cells_n, lanes), 0).astype(jnp.float32)


def sample_group(g, part_row, cells, block_of, tile_of, p_ref, u_ref, state_ref, rows, sp, su, sn):
    _, lanes = cells.shape
    base = g * GROUP
    for j in range(GROUP):
        tile = tile_of(base + j)
        state_ref[pl.ds(g * ROWS + j, STATES, stride=GROUP), :] = block_of(base + j)
        at = part_row + 4 * j
        rows[at : at + 1, :] = p_ref[0, pl.ds(tile, 1), :]
        rows[at + 1 : at + 2, :] = u_ref[0, pl.ds(tile, 1), :]
    for pair in range(GROUP // 2):
        highs, lows = [], []
        for j in (2 * pair, 2 * pair + 1):
            position = state_ref[pl.ds(g * ROWS + 2 * GROUP + j, 1), :]
            high, low = split_bf16(raw_weights(position, cells))
            highs.append(high)
            lows.append(low)
        rhs = jnp.concatenate(
            [jnp.concatenate(highs, axis=1), jnp.concatenate(lows, axis=1)], axis=0
        )
        lhs = stacked_lhs(rows[part_row + 8 * pair : part_row + 8 * pair + 8, :])
        result = jnp.dot(lhs, rhs, preferred_element_type=jnp.float32)
        result = result[:8] + result[8:]
        for side in range(2):
            part = result[:, side * lanes : (side + 1) * lanes]
            at = base + 2 * pair + side
            sp[pl.ds(at, 1), :] = part[4 * side : 4 * side + 1]
            su[pl.ds(at, 1), :] = part[4 * side + 1 : 4 * side + 2]
            sn[pl.ds(at, 1), :] = part[2:3]


def clear_rows(rows):
    rows[...] = jnp.zeros_like(rows)
    for pair in range(rows.shape[0] // 8):
        rows[8 * pair + 2 : 8 * pair + 3, :] = jnp.ones((1, rows.shape[1]), jnp.float32)


def advance_group(g, state_ref, sp, su, sn, live):
    row = pl.multiple_of(g * GROUP, GROUP)
    at = [pl.multiple_of(g * ROWS + c * GROUP, GROUP) for c in range(STATES)]
    radius, growth, position, speed, rest = (state_ref[pl.ds(a, GROUP), :] for a in at)
    if live is None:
        live = radius * rest >= 0.0
        radius = jnp.where(live, radius, 1.0)
    inverse = 1.0 / sn[pl.ds(row, GROUP), :]
    pressure = sp[pl.ds(row, GROUP), :] * inverse
    velocity = su[pl.ds(row, GROUP), :] * inverse
    drive = AMBIENT + PRESSURE_COUPLING * pressure
    h = TIME_STEP / SUBSTEPS
    for _ in range(SUBSTEPS):
        over = 1.0 / radius
        gas = jnp.exp(GAS_INDEX * jnp.log(rest * over))
        accel = (gas - drive - 1.5 * growth * growth - VISCOUS * growth * over) * over
        growth = growth + h * accel
        radius = radius + h * growth
        speed = speed + (h / RELAX_TIME) * (velocity - speed)
        position = position + h * speed
    return at, live, (radius, growth, position, speed, rest)


def spread_group(g, cells, tile_of, position_ref, amounts, source_ref, void_ref):
    cells_n, lanes = cells.shape
    base = g * GROUP
    sublane = lax.broadcasted_iota(jnp.int32, (8, lanes), 0)
    for pair in range(GROUP // 2):
        pieces, norms = [], []
        for j in (2 * pair, 2 * pair + 1):
            position = position_ref[pl.ds(g * ROWS + 2 * GROUP + j, 1), :]
            raw = raw_weights(position, cells)
            norms.append(jnp.sum(raw, axis=0, keepdims=True))
            pieces.append(jnp.concatenate(split_bf16(raw), axis=1))
        rhs = jnp.concatenate(pieces, axis=0)
        amount = amounts[pl.ds(pl.multiple_of(g * 4 * GROUP + 8 * pair, 8), 8), :]
        amount = amount / jnp.where(sublane < 4, norms[0], norms[1])
        result = lax.dot_general(
            stacked_lhs(amount), rhs, (((1,), (1,)), ((), ())),
            preferred_element_type=jnp.float32,
        )
        result = result[:8] + result[8:]
        for side in range(2):
            part = result[:, side * cells_n : (side + 1) * cells_n]
            tile = tile_of(base + 2 * pair + side)
            source_ref[pl.ds(tile, 1), :] += part[4 * side : 4 * side + 1]
            if void_ref is not None:
                void_ref[pl.ds(tile, 1), :] += part[4 * side + 1 : 4 * side + 2]


def set_amounts(g, amounts, live, radius, growth, void):
    at = g * 4 * GROUP
    source = SOURCE_GAIN * FOUR_PI * radius * radius * growth
    amounts[pl.ds(at, GROUP, stride=4), :] = jnp.where(live, source, 0.0)
    if void:
        volume = VOID_SCALE * FOUR_PI / 3.0 * radius * radius * radius
        amounts[pl.ds(at + 1, GROUP, stride=4), :] = jnp.where(live, volume, 0.0)


def first_kernel(order_ref, tiles_ref, count_ref, bubbles_ref, p_ref, u_ref, after,
                 state_ref, amounts, sp, su, sn, rows):
    cells_n, lanes = p_ref.shape[-1], sp.shape[1]
    slots = sp.shape[0]
    groups = slots // GROUP
    cells = cell_centres(cells_n, lanes)
    clear_rows(rows)
    amounts[...] = jnp.zeros_like(amounts)
    state_row = lax.broadcasted_iota(jnp.int32, (STATES, lanes), 0)
    marker = jnp.where(state_row == 0, -1.0, 1.0)

    def block_of(slot):
        block = order_ref[slot]
        state = jnp.concatenate(
            [bubbles_ref[pl.ds(c * slots + block, 1), :] for c in range(STATES)], axis=0
        )
        return jnp.where(block < count_ref[0], state, marker)

    def sample(w, carry):
        for i in range(UNROLL):
            sample_group(w * UNROLL + i, 4 * GROUP * i, cells, block_of,
                         lambda slot: tiles_ref[order_ref[slot]],
                         p_ref, u_ref, state_ref, rows, sp, su, sn)
        return carry

    def advance(w, carry):
        for i in range(WIDE):
            g = w * WIDE + i
            at, live, new = advance_group(g, state_ref, sp, su, sn, None)
            set_amounts(g, amounts, live, new[0], new[1], False)
            new = (jnp.where(live, new[0], -1.0),) + new[1:]
            for a, x in zip(at, new):
                state_ref[pl.ds(a, GROUP), :] = x
        return carry

    lax.fori_loop(0, groups // UNROLL, sample, 0)
    lax.fori_loop(0, groups // WIDE, advance, 0)


def spread_kernel(order_ref, tiles_ref, state_ref, amounts, source_ref):
    cells = cell_centres(source_ref.shape[1], amounts.shape[1])
    source_ref[...] = jnp.zeros_like(source_ref)

    def spread(w, carry):
        for i in range(UNROLL):
            spread_group(w * UNROLL + i, cells, lambda slot: tiles_ref[order_ref[slot]],
                         state_ref, amounts, source_ref, None)
        return carry

    lax.fori_loop(0, amounts.shape[0] // (4 * GROUP * UNROLL), spread, 0)


def second_kernel(live_ref, tiles_ref, arrived_ref, p_ref, u_ref,
                  bubbles_out, source_ref, void_ref, sp, su, sn, rows, amounts, state_ref, list_ref):
    cells_n, lanes = p_ref.shape[-1], sp.shape[1]
    slots = sp.shape[0]
    cells = cell_centres(cells_n, lanes)
    clear_rows(rows)
    for ref in (bubbles_out, source_ref, void_ref, amounts):
        ref[...] = jnp.zeros_like(ref)

    def keep(i, n):
        for k in range(GROUP):
            list_ref[n] = i * GROUP + k
            n = n + live_ref[i * GROUP + k]
        return n

    number = lax.fori_loop(0, slots // GROUP, keep, 0)
    chunk = GROUP * WIDE
    chunks = (number + chunk - 1) // chunk

    def pad(i, carry):
        list_ref[i] = list_ref[0]
        return carry

    lax.fori_loop(number, chunks * chunk, pad, 0)

    def block_of(entry):
        slot = list_ref[entry]
        at = slot // GROUP * ROWS + slot % GROUP
        return arrived_ref[pl.ds(at, STATES, stride=GROUP), :]

    def tile_of(entry):
        return tiles_ref[list_ref[entry]]

    def sample(w, carry):
        for i in range(UNROLL):
            sample_group(w * UNROLL + i, 4 * GROUP * i, cells, block_of, tile_of,
                         p_ref, u_ref, state_ref, rows, sp, su, sn)
        return carry

    def advance(w, carry):
        for i in range(WIDE):
            g = w * WIDE + i
            entry = g * GROUP + lax.broadcasted_iota(jnp.int32, (GROUP, lanes), 0)
            at, live, new = advance_group(g, state_ref, sp, su, sn, entry < number)
            set_amounts(g, amounts, live, new[0], new[1], True)
            for a, x in zip(at, new):
                state_ref[pl.ds(a, GROUP), :] = x
        return carry

    def spread(w, carry):
        for i in range(UNROLL):
            g = w * UNROLL + i
            spread_group(g, cells, tile_of, state_ref, amounts, source_ref, void_ref)
            for j in range(GROUP):
                slot = list_ref[g * GROUP + j]
                state = state_ref[pl.ds(g * ROWS + j, STATES, stride=GROUP), :]
                for c in range(STATES):
                    bubbles_out[pl.ds(c * slots + slot, 1), :] = state[c : c + 1]
        return carry

    lax.fori_loop(0, chunks * (WIDE // UNROLL), sample, 0)
    lax.fori_loop(0, chunks, advance, 0)
    lax.fori_loop(0, chunks * (WIDE // UNROLL), spread, 0)


VMEM_GRANT = 60 * 2**20


def whole(shape):
    return pl.BlockSpec(tuple(shape), lambda i: (0,) * len(shape))


def call(kernel, scalars, arrays, specs, outs, scratch, passes, work):
    return pl.pallas_call(
        kernel,
        grid=(1,),
        out_shape=outs,
        in_specs=[pl.BlockSpec(memory_space=pltpu.SMEM)] * len(scalars) + specs,
        out_specs=tuple(whole(o.shape) for o in outs),
        scratch_shapes=scratch,
        compiler_params=pltpu.CompilerParams(vmem_limit_bytes=VMEM_GRANT),
        cost_estimate=pl.CostEstimate(
            flops=work * 1000 * passes, bytes_accessed=6 * 2**20, transcendentals=passes * work
        ),
    )(*scalars, *arrays)


def f32(*shape):
    return jax.ShapeDtypeStruct(shape, jnp.float32)


def flow_specs(tiles, cells):
    return [
        pl.BlockSpec((1, tiles, cells), lambda i: (0, 0, 0)),
        pl.BlockSpec((1, tiles, cells), lambda i: (3, 0, 0)),
    ]


def sample_and_advance(fluid, order, tiles_ids, counts, bubbles, after):
    _, tiles, cells = fluid.shape
    slots, lanes = order.shape[0], bubbles.shape[1]
    scratch = [pltpu.VMEM((slots, lanes), jnp.float32) for _ in range(3)]
    scratch.append(pltpu.VMEM((4 * GROUP * UNROLL, cells), jnp.float32))
    return call(
        first_kernel, (order, tiles_ids, counts), (bubbles, fluid, fluid, after),
        [whole(bubbles.shape)] + flow_specs(tiles, cells) + [pl.BlockSpec(memory_space=pl.ANY)],
        (f32(slots * STATES, lanes), f32(4 * slots, lanes)),
        scratch, 1, slots * lanes * cells,
    )


def spread_first(tiles, cells, order, tiles_ids, state, amounts):
    work = order.shape[0] * state.shape[1] * cells
    (source,) = call(
        spread_kernel, (order, tiles_ids), (state, amounts),
        [whole(state.shape), whole(amounts.shape)], (f32(tiles, cells),), [], 1, work,
    )
    return source


def bubbles_second(fluid, live, tiles_ids, arrived):
    _, tiles, cells = fluid.shape
    slots, lanes = tiles_ids.shape[0], arrived.shape[1]
    scratch = [pltpu.VMEM((slots, lanes), jnp.float32) for _ in range(3)]
    scratch += [
        pltpu.VMEM((4 * GROUP * UNROLL, cells), jnp.float32),
        pltpu.VMEM((4 * slots, lanes), jnp.float32),
        pltpu.VMEM((slots * STATES, lanes), jnp.float32),
        pltpu.SMEM((slots + GROUP * WIDE,), jnp.int32),
    ]
    return call(
        second_kernel, (live, tiles_ids), (arrived, fluid, fluid),
        [whole(arrived.shape)] + flow_specs(tiles, cells),
        (f32(STATES * slots, lanes), f32(tiles, cells), f32(tiles, cells)),
        scratch, 2, slots * lanes * cells,
    )


def fluid_kernel(edges, f_ref, before_ref, after_ref, low_ref, high_ref, left_ref, right_ref,
                 source_ref, out_ref, *edge_refs):
    step, steps = pl.program_id(0), pl.num_programs(0)
    comps, depth, width, cells = f_ref.shape
    row = lax.broadcasted_iota(jnp.int32, (width, cells), 0)
    lane = lax.broadcasted_iota(jnp.int32, (width, cells), 1)
    at_start, at_end = step == 0, step == steps - 1
    for s in range(depth):
        now, below, above = [], [], []
        for c in range(comps):
            now.append(f_ref[c, s])
            below.append(
                jnp.where(at_start, low_ref[c, 0], before_ref[c, 0]) if s == 0 else f_ref[c, s - 1]
            )
            above.append(
                jnp.where(at_end, high_ref[c, 0], after_ref[c, 0])
                if s == depth - 1
                else f_ref[c, s + 1]
            )
        d_s, d_a, d_r, lap = [], [], [], []
        for c in range(comps):
            x = now[c]
            a_down = jnp.where(row == 0, left_ref[c, s : s + 1, :], pltpu.roll(x, 1, 0))
            a_up = jnp.where(
                row == width - 1, right_ref[c, s : s + 1, :], pltpu.roll(x, width - 1, 0)
            )
            r_down = jnp.where(lane == 0, 0.0, pltpu.roll(x, 1, 1))
            r_up = jnp.where(lane == cells - 1, 0.0, pltpu.roll(x, cells - 1, 1))
            d_s.append(above[c] - below[c])
            d_a.append(a_up - a_down)
            d_r.append(r_up - r_down)
            lap.append(above[c] + below[c] + a_up + a_down + r_up + r_down - 6.0 * x)
        half = 0.5 * TIME_STEP
        change = [
            MEAN_FLOW * d_s[0] + d_s[1] + d_a[2] + d_r[3],
            MEAN_FLOW * d_s[1] + d_s[0],
            MEAN_FLOW * d_s[2] + d_a[0],
            MEAN_FLOW * d_s[3] + d_r[0],
        ]
        for c in range(comps):
            new = now[c] - half * change[c] + DIFFUSION * lap[c]
            if c == 0:
                new = new - TIME_STEP * source_ref[s]
            out_ref[c, s] = new
            if edges:
                edge_refs[0][c, s : s + 1, :] = new[0:1]
                edge_refs[1][c, s : s + 1, :] = new[width - 1 : width]


def fluid_step(edges, fluid, halos, source):
    comps, length, width, cells = fluid.shape
    depth = 16
    steps = length // depth
    plane = (comps, 1, width, cells)
    side = pl.BlockSpec((comps, depth, cells), lambda i: (0, i, 0))
    still = pl.BlockSpec(plane, lambda i: (0, 0, 0, 0))
    main = pl.BlockSpec((comps, depth, width, cells), lambda i: (0, i, 0, 0))
    outs = [jax.ShapeDtypeStruct(fluid.shape, jnp.float32)]
    out_specs = [main]
    if edges:
        outs += [jax.ShapeDtypeStruct((comps, length, cells), jnp.float32)] * 2
        out_specs += [side, side]
    return pl.pallas_call(
        functools.partial(fluid_kernel, edges),
        grid=(steps,),
        out_shape=tuple(outs),
        in_specs=[
            main,
            pl.BlockSpec(plane, lambda i: (0, jnp.maximum(i * depth - 1, 0), 0, 0)),
            pl.BlockSpec(plane, lambda i: (0, jnp.minimum(i * depth + depth, length - 1), 0, 0)),
            still,
            still,
            side,
            side,
            pl.BlockSpec((depth, width, cells), lambda i: (i, 0, 0)),
        ],
        out_specs=tuple(out_specs),
        compiler_params=pltpu.CompilerParams(vmem_limit_bytes=VMEM_GRANT),
        cost_estimate=pl.CostEstimate(
            flops=fluid.size * 30, bytes_accessed=10 * 2**20, transcendentals=0
        ),
        name="fluid_first" if edges else "fluid_second",
    )(fluid, fluid, fluid, *halos, source)


def exchange_kernel(after, *refs):
    first_plane, last_plane, first_col, last_col = refs[:4]
    low, high, left, right, send, recv = refs[4 + after :]
    streams, azims = lax.axis_size("stream"), lax.axis_size("azim")
    s, a = lax.axis_index("stream"), lax.axis_index("azim")
    targets = (
        (lax.rem(s + 1, streams), a),
        (lax.rem(s + streams - 1, streams), a),
        (s, lax.rem(a + 1, azims)),
        (s, lax.rem(a + azims - 1, azims)),
    )
    barrier = pltpu.get_barrier_semaphore()
    for target in targets:
        pl.semaphore_signal(
            barrier, inc=1, device_id=target, device_id_type=pl.DeviceIdType.MESH
        )
    pl.semaphore_wait(barrier, len(targets))
    ends = ((last_plane, low), (first_plane, high), (last_col, left), (first_col, right))
    copies = []
    for i, ((source, landing), target) in enumerate(zip(ends, targets)):
        copies.append(
            pltpu.make_async_remote_copy(
                src_ref=source,
                dst_ref=landing,
                send_sem=send.at[i],
                recv_sem=recv.at[i],
                device_id=target,
                device_id_type=pl.DeviceIdType.MESH,
            )
        )
    for copy in copies:
        copy.start()
    for copy in copies:
        copy.wait()

    @pl.when(s == 0)
    def _():
        low[...] = jnp.zeros_like(low)

    @pl.when(s == streams - 1)
    def _():
        high[...] = jnp.zeros_like(high)


def exchange(number, fluid, first_col, last_col, *after):
    planes = (fluid[:, :1], fluid[:, fluid.shape[1] - 1 :])
    vmem = pl.BlockSpec(memory_space=pltpu.VMEM)
    plane, column = f32(*planes[0].shape), f32(*first_col.shape)
    return pl.pallas_call(
        functools.partial(exchange_kernel, len(after)),
        out_shape=(plane, plane, column, column),
        in_specs=[vmem] * 4 + [pl.BlockSpec(memory_space=pl.ANY)] * len(after),
        out_specs=(vmem,) * 4,
        scratch_shapes=[pltpu.SemaphoreType.DMA((4,)), pltpu.SemaphoreType.DMA((4,))],
        compiler_params=pltpu.CompilerParams(
            collective_id=number, has_side_effects=True, vmem_limit_bytes=VMEM_GRANT
        ),
    )(*planes, first_col, last_col, *after)


def on_device(fluid, bubbles, counts, outgoing_block_order, tiles_first_update, tiles_after):
    comps, length, width, cells = fluid.shape
    slots, states, lanes = bubbles.shape
    devices = lax.axis_size("stream") * lax.axis_size("azim")
    cap = slots // devices
    flat = (comps, length * width, cells)
    grid = (length, width, cells)
    axes = ("stream", "azim")
    bubbles = bubbles.transpose(1, 0, 2).reshape(states * slots, lanes)
    halos = exchange(0, fluid, fluid[:, :, 0], fluid[:, :, width - 1])
    state, amounts = sample_and_advance(
        fluid.reshape(flat), outgoing_block_order, tiles_first_update, counts, bubbles, halos[0]
    )
    sent = state
    if cap % GROUP:
        sent = sent.reshape(slots // GROUP, states, GROUP, lanes).transpose(0, 2, 1, 3)
    arrived = lax.all_to_all(
        sent.reshape(devices, cap * states, lanes), axes,
        split_axis=0, concat_axis=0, tiled=True,
    )
    if cap % GROUP:
        arrived = arrived.reshape(slots // GROUP, GROUP, states, lanes).transpose(0, 2, 1, 3)
    arrived = arrived.reshape(slots // GROUP, states, GROUP, lanes)
    live = (arrived[:, 0, :, 0] * arrived[:, 4, :, 0] >= 0.0).astype(jnp.int32).reshape(slots)
    source = spread_first(
        length * width, cells, outgoing_block_order, tiles_first_update, state, amounts
    )
    fluid, first_col, last_col = fluid_step(True, fluid, halos, source.reshape(grid))
    bubbles, source, void = bubbles_second(
        fluid.reshape(flat), live, tiles_after, arrived.reshape(slots * states, lanes)
    )
    halos = exchange(1, fluid, first_col, last_col, source)
    (fluid,) = fluid_step(False, fluid, halos, source.reshape(grid))
    bubbles = bubbles.reshape(states, slots, lanes).transpose(1, 0, 2)
    return fluid, bubbles, void.reshape(grid)


def solution(mesh):
    return jax.shard_map(
        on_device,
        mesh=mesh,
        in_specs=(
            P(None, "stream", "azim", None),
            P(("stream", "azim"), None, None),
            P(("stream", "azim")),
            P(("stream", "azim")),
            P(("stream", "azim")),
            P(("stream", "azim")),
        ),
        out_specs=(
            P(None, "stream", "azim", None),
            P(("stream", "azim"), None, None),
            P("stream", "azim", None),
        ),
        check_vma=False,
    )
```

```python
import functools

import jax
import jax.numpy as jnp
from jax import lax
from jax.experimental import pallas as pl
from jax.experimental.pallas import tpu as pltpu
from jax.sharding import PartitionSpec as P


SUBSTEPS = 8
TIME_STEP = 0.25
MEAN_FLOW = 0.5
DIFFUSION = 0.1
KERNEL_WIDTH = 1.5
GAS_INDEX = 4.2
PRESSURE_COUPLING = 0.3
AMBIENT = 1.0
RELAX_TIME = 0.5
VISCOUS = 0.08
SOURCE_GAIN = 0.05
VOID_SCALE = 0.01
FOUR_PI = 12.566370614359172
LOG2E = 1.4426950408889634
GROUP = 8
STATES = 5
ROWS = GROUP * STATES
WIDE = 4
UNROLL = 4


def split_bf16(values):
    high = values.astype(jnp.bfloat16)
    low = (values - high.astype(jnp.float32)).astype(jnp.bfloat16)
    return high, low


def stacked_lhs(rows):
    high = rows.astype(jnp.bfloat16).astype(jnp.float32)
    both = jnp.concatenate([high, rows - high], axis=0).astype(jnp.bfloat16)
    return jnp.concatenate([both, both], axis=1)


def raw_weights(position_row, cells):
    offset = cells - position_row
    return jnp.exp2(offset * offset * (-0.5 * LOG2E / (KERNEL_WIDTH * KERNEL_WIDTH)))


def cell_centres(cells_n, lanes):
    return lax.broadcasted_iota(jnp.int32, (cells_n, lanes), 0).astype(jnp.float32)


def sample_group(g, part_row, cells, block_of, tile_of, p_ref, u_ref, state_ref, rows, sp, su, sn):
    _, lanes = cells.shape
    base = g * GROUP
    for j in range(GROUP):
        tile = tile_of(base + j)
        state_ref[pl.ds(g * ROWS + j, STATES, stride=GROUP), :] = block_of(base + j)
        at = part_row + 4 * j
        rows[at : at + 1, :] = p_ref[0, pl.ds(tile, 1), :]
        rows[at + 1 : at + 2, :] = u_ref[0, pl.ds(tile, 1), :]
    for pair in range(GROUP // 2):
        highs, lows = [], []
        for j in (2 * pair, 2 * pair + 1):
            position = state_ref[pl.ds(g * ROWS + 2 * GROUP + j, 1), :]
            high, low = split_bf16(raw_weights(position, cells))
            highs.append(high)
            lows.append(low)
        rhs = jnp.concatenate(
            [jnp.concatenate(highs, axis=1), jnp.concatenate(lows, axis=1)], axis=0
        )
        lhs = stacked_lhs(rows[part_row + 8 * pair : part_row + 8 * pair + 8, :])
        result = jnp.dot(lhs, rhs, preferred_element_type=jnp.float32)
        result = result[:8] + result[8:]
        for side in range(2):
            part = result[:, side * lanes : (side + 1) * lanes]
            at = base + 2 * pair + side
            sp[pl.ds(at, 1), :] = part[4 * side : 4 * side + 1]
            su[pl.ds(at, 1), :] = part[4 * side + 1 : 4 * side + 2]
            sn[pl.ds(at, 1), :] = part[2:3]


def clear_rows(rows):
    rows[...] = jnp.zeros_like(rows)
    for pair in range(rows.shape[0] // 8):
        rows[8 * pair + 2 : 8 * pair + 3, :] = jnp.ones((1, rows.shape[1]), jnp.float32)


def advance_group(g, state_ref, sp, su, sn, live):
    row = pl.multiple_of(g * GROUP, GROUP)
    at = [pl.multiple_of(g * ROWS + c * GROUP, GROUP) for c in range(STATES)]
    radius, growth, position, speed, rest = (state_ref[pl.ds(a, GROUP), :] for a in at)
    if live is None:
        live = radius * rest >= 0.0
        radius = jnp.where(live, radius, 1.0)
    inverse = 1.0 / sn[pl.ds(row, GROUP), :]
    pressure = sp[pl.ds(row, GROUP), :] * inverse
    velocity = su[pl.ds(row, GROUP), :] * inverse
    drive = AMBIENT + PRESSURE_COUPLING * pressure
    h = TIME_STEP / SUBSTEPS
    for _ in range(SUBSTEPS):
        over = 1.0 / radius
        gas = jnp.exp(GAS_INDEX * jnp.log(rest * over))
        accel = (gas - drive - 1.5 * growth * growth - VISCOUS * growth * over) * over
        growth = growth + h * accel
        radius = radius + h * growth
        speed = speed + (h / RELAX_TIME) * (velocity - speed)
        position = position + h * speed
    return at, live, (radius, growth, position, speed, rest)


def spread_group(g, cells, tile_of, position_ref, amounts, source_ref, void_ref):
    cells_n, lanes = cells.shape
    base = g * GROUP
    sublane = lax.broadcasted_iota(jnp.int32, (8, lanes), 0)
    for pair in range(GROUP // 2):
        pieces, norms = [], []
        for j in (2 * pair, 2 * pair + 1):
            position = position_ref[pl.ds(g * ROWS + 2 * GROUP + j, 1), :]
            raw = raw_weights(position, cells)
            norms.append(jnp.sum(raw, axis=0, keepdims=True))
            pieces.append(jnp.concatenate(split_bf16(raw), axis=1))
        rhs = jnp.concatenate(pieces, axis=0)
        amount = amounts[pl.ds(pl.multiple_of(g * 4 * GROUP + 8 * pair, 8), 8), :]
        amount = amount / jnp.where(sublane < 4, norms[0], norms[1])
        result = lax.dot_general(
            stacked_lhs(amount), rhs, (((1,), (1,)), ((), ())),
            preferred_element_type=jnp.float32,
        )
        result = result[:8] + result[8:]
        for side in range(2):
            part = result[:, side * cells_n : (side + 1) * cells_n]
            tile = tile_of(base + 2 * pair + side)
            source_ref[pl.ds(tile, 1), :] += part[4 * side : 4 * side + 1]
            if void_ref is not None:
                void_ref[pl.ds(tile, 1), :] += part[4 * side + 1 : 4 * side + 2]


def set_amounts(g, amounts, live, radius, growth, void):
    at = g * 4 * GROUP
    source = SOURCE_GAIN * FOUR_PI * radius * radius * growth
    amounts[pl.ds(at, GROUP, stride=4), :] = jnp.where(live, source, 0.0)
    if void:
        volume = VOID_SCALE * FOUR_PI / 3.0 * radius * radius * radius
        amounts[pl.ds(at + 1, GROUP, stride=4), :] = jnp.where(live, volume, 0.0)


def first_kernel(order_ref, tiles_ref, count_ref, bubbles_ref, p_ref, u_ref,
                 state_ref, amounts, sp, su, sn, rows):
    cells_n, lanes = p_ref.shape[-1], sp.shape[1]
    slots = sp.shape[0]
    groups = slots // GROUP
    cells = cell_centres(cells_n, lanes)
    clear_rows(rows)
    amounts[...] = jnp.zeros_like(amounts)
    state_row = lax.broadcasted_iota(jnp.int32, (STATES, lanes), 0)
    marker = jnp.where(state_row == 0, -1.0, 1.0)

    def block_of(slot):
        block = order_ref[slot]
        state = jnp.concatenate(
            [bubbles_ref[pl.ds(c * slots + block, 1), :] for c in range(STATES)], axis=0
        )
        return jnp.where(block < count_ref[0], state, marker)

    def sample(w, carry):
        for i in range(UNROLL):
            sample_group(w * UNROLL + i, 4 * GROUP * i, cells, block_of,
                         lambda slot: tiles_ref[order_ref[slot]],
                         p_ref, u_ref, state_ref, rows, sp, su, sn)
        return carry

    def advance(w, carry):
        for i in range(WIDE):
            g = w * WIDE + i
            at, live, new = advance_group(g, state_ref, sp, su, sn, None)
            set_amounts(g, amounts, live, new[0], new[1], False)
            new = (jnp.where(live, new[0], -1.0),) + new[1:]
            for a, x in zip(at, new):
                state_ref[pl.ds(a, GROUP), :] = x
        return carry

    lax.fori_loop(0, groups // UNROLL, sample, 0)
    lax.fori_loop(0, groups // WIDE, advance, 0)


def spread_kernel(order_ref, tiles_ref, state_ref, amounts, source_ref):
    cells = cell_centres(source_ref.shape[1], amounts.shape[1])
    source_ref[...] = jnp.zeros_like(source_ref)

    def spread(w, carry):
        for i in range(UNROLL):
            spread_group(w * UNROLL + i, cells, lambda slot: tiles_ref[order_ref[slot]],
                         state_ref, amounts, source_ref, None)
        return carry

    lax.fori_loop(0, amounts.shape[0] // (4 * GROUP * UNROLL), spread, 0)


def second_kernel(live_ref, tiles_ref, arrived_ref, p_ref, u_ref,
                  bubbles_out, source_ref, void_ref, sp, su, sn, rows, amounts, state_ref, list_ref):
    cells_n, lanes = p_ref.shape[-1], sp.shape[1]
    slots = sp.shape[0]
    cells = cell_centres(cells_n, lanes)
    clear_rows(rows)
    for ref in (bubbles_out, source_ref, void_ref, amounts):
        ref[...] = jnp.zeros_like(ref)

    def keep(i, n):
        for k in range(GROUP):
            list_ref[n] = i * GROUP + k
            n = n + live_ref[i * GROUP + k]
        return n

    number = lax.fori_loop(0, slots // GROUP, keep, 0)
    chunk = GROUP * WIDE
    chunks = (number + chunk - 1) // chunk

    def pad(i, carry):
        list_ref[i] = list_ref[0]
        return carry

    lax.fori_loop(number, chunks * chunk, pad, 0)

    def block_of(entry):
        slot = list_ref[entry]
        at = slot // GROUP * ROWS + slot % GROUP
        return arrived_ref[pl.ds(at, STATES, stride=GROUP), :]

    def tile_of(entry):
        return tiles_ref[list_ref[entry]]

    def sample(w, carry):
        for i in range(UNROLL):
            sample_group(w * UNROLL + i, 4 * GROUP * i, cells, block_of, tile_of,
                         p_ref, u_ref, state_ref, rows, sp, su, sn)
        return carry

    def advance(w, carry):
        for i in range(WIDE):
            g = w * WIDE + i
            entry = g * GROUP + lax.broadcasted_iota(jnp.int32, (GROUP, lanes), 0)
            at, live, new = advance_group(g, state_ref, sp, su, sn, entry < number)
            set_amounts(g, amounts, live, new[0], new[1], True)
            for a, x in zip(at, new):
                state_ref[pl.ds(a, GROUP), :] = x
        return carry

    def spread(w, carry):
        for i in range(UNROLL):
            g = w * UNROLL + i
            spread_group(g, cells, tile_of, state_ref, amounts, source_ref, void_ref)
            for j in range(GROUP):
                slot = list_ref[g * GROUP + j]
                state = state_ref[pl.ds(g * ROWS + j, STATES, stride=GROUP), :]
                for c in range(STATES):
                    bubbles_out[pl.ds(c * slots + slot, 1), :] = state[c : c + 1]
        return carry

    lax.fori_loop(0, chunks * (WIDE // UNROLL), sample, 0)
    lax.fori_loop(0, chunks, advance, 0)
    lax.fori_loop(0, chunks * (WIDE // UNROLL), spread, 0)


VMEM_GRANT = 60 * 2**20


def whole(shape):
    return pl.BlockSpec(tuple(shape), lambda i: (0,) * len(shape))


def call(kernel, scalars, arrays, specs, outs, scratch, passes, work):
    return pl.pallas_call(
        kernel,
        grid=(1,),
        out_shape=outs,
        in_specs=[pl.BlockSpec(memory_space=pltpu.SMEM)] * len(scalars) + specs,
        out_specs=tuple(whole(o.shape) for o in outs),
        scratch_shapes=scratch,
        compiler_params=pltpu.CompilerParams(vmem_limit_bytes=VMEM_GRANT),
        cost_estimate=pl.CostEstimate(
            flops=work * 1000 * passes, bytes_accessed=6 * 2**20, transcendentals=passes * work
        ),
    )(*scalars, *arrays)


def f32(*shape):
    return jax.ShapeDtypeStruct(shape, jnp.float32)


def flow_specs(tiles, cells):
    return [
        pl.BlockSpec((1, tiles, cells), lambda i: (0, 0, 0)),
        pl.BlockSpec((1, tiles, cells), lambda i: (3, 0, 0)),
    ]


def sample_and_advance(fluid, order, tiles_ids, counts, bubbles):
    _, tiles, cells = fluid.shape
    slots, lanes = order.shape[0], bubbles.shape[1]
    scratch = [pltpu.VMEM((slots, lanes), jnp.float32) for _ in range(3)]
    scratch.append(pltpu.VMEM((4 * GROUP * UNROLL, cells), jnp.float32))
    return call(
        first_kernel, (order, tiles_ids, counts), (bubbles, fluid, fluid),
        [whole(bubbles.shape)] + flow_specs(tiles, cells),
        (f32(slots * STATES, lanes), f32(4 * slots, lanes)),
        scratch, 1, slots * lanes * cells,
    )


def spread_first(tiles, cells, order, tiles_ids, state, amounts):
    work = order.shape[0] * state.shape[1] * cells
    (source,) = call(
        spread_kernel, (order, tiles_ids), (state, amounts),
        [whole(state.shape), whole(amounts.shape)], (f32(tiles, cells),), [], 1, work,
    )
    return source


def bubbles_second(fluid, live, tiles_ids, arrived):
    _, tiles, cells = fluid.shape
    slots, lanes = tiles_ids.shape[0], arrived.shape[1]
    scratch = [pltpu.VMEM((slots, lanes), jnp.float32) for _ in range(3)]
    scratch += [
        pltpu.VMEM((4 * GROUP * UNROLL, cells), jnp.float32),
        pltpu.VMEM((4 * slots, lanes), jnp.float32),
        pltpu.VMEM((slots * STATES, lanes), jnp.float32),
        pltpu.SMEM((slots + GROUP * WIDE,), jnp.int32),
    ]
    return call(
        second_kernel, (live, tiles_ids), (arrived, fluid, fluid),
        [whole(arrived.shape)] + flow_specs(tiles, cells),
        (f32(STATES * slots, lanes), f32(tiles, cells), f32(tiles, cells)),
        scratch, 2, slots * lanes * cells,
    )


def fluid_kernel(edges, f_ref, before_ref, after_ref, low_ref, high_ref, left_ref, right_ref,
                 source_ref, out_ref, *edge_refs):
    step, steps = pl.program_id(0), pl.num_programs(0)
    comps, depth, width, cells = f_ref.shape
    row = lax.broadcasted_iota(jnp.int32, (width, cells), 0)
    lane = lax.broadcasted_iota(jnp.int32, (width, cells), 1)
    at_start, at_end = step == 0, step == steps - 1
    for s in range(depth):
        now, below, above = [], [], []
        for c in range(comps):
            now.append(f_ref[c, s])
            below.append(
                jnp.where(at_start, low_ref[c, 0], before_ref[c, 0]) if s == 0 else f_ref[c, s - 1]
            )
            above.append(
                jnp.where(at_end, high_ref[c, 0], after_ref[c, 0])
                if s == depth - 1
                else f_ref[c, s + 1]
            )
        d_s, d_a, d_r, lap = [], [], [], []
        for c in range(comps):
            x = now[c]
            a_down = jnp.where(row == 0, left_ref[c, s : s + 1, :], pltpu.roll(x, 1, 0))
            a_up = jnp.where(
                row == width - 1, right_ref[c, s : s + 1, :], pltpu.roll(x, width - 1, 0)
            )
            r_down = jnp.where(lane == 0, 0.0, pltpu.roll(x, 1, 1))
            r_up = jnp.where(lane == cells - 1, 0.0, pltpu.roll(x, cells - 1, 1))
            d_s.append(above[c] - below[c])
            d_a.append(a_up - a_down)
            d_r.append(r_up - r_down)
            lap.append(above[c] + below[c] + a_up + a_down + r_up + r_down - 6.0 * x)
        half = 0.5 * TIME_STEP
        change = [
            MEAN_FLOW * d_s[0] + d_s[1] + d_a[2] + d_r[3],
            MEAN_FLOW * d_s[1] + d_s[0],
            MEAN_FLOW * d_s[2] + d_a[0],
            MEAN_FLOW * d_s[3] + d_r[0],
        ]
        for c in range(comps):
            new = now[c] - half * change[c] + DIFFUSION * lap[c]
            if c == 0:
                new = new - TIME_STEP * source_ref[s]
            out_ref[c, s] = new
            if edges:
                edge_refs[0][c, s : s + 1, :] = new[0:1]
                edge_refs[1][c, s : s + 1, :] = new[width - 1 : width]


def fluid_step(edges, fluid, halos, source):
    comps, length, width, cells = fluid.shape
    depth = 16
    steps = length // depth
    plane = (comps, 1, width, cells)
    side = pl.BlockSpec((comps, depth, cells), lambda i: (0, i, 0))
    still = pl.BlockSpec(plane, lambda i: (0, 0, 0, 0))
    main = pl.BlockSpec((comps, depth, width, cells), lambda i: (0, i, 0, 0))
    outs = [jax.ShapeDtypeStruct(fluid.shape, jnp.float32)]
    out_specs = [main]
    if edges:
        outs += [jax.ShapeDtypeStruct((comps, length, cells), jnp.float32)] * 2
        out_specs += [side, side]
    return pl.pallas_call(
        functools.partial(fluid_kernel, edges),
        grid=(steps,),
        out_shape=tuple(outs),
        in_specs=[
            main,
            pl.BlockSpec(plane, lambda i: (0, jnp.maximum(i * depth - 1, 0), 0, 0)),
            pl.BlockSpec(plane, lambda i: (0, jnp.minimum(i * depth + depth, length - 1), 0, 0)),
            still,
            still,
            side,
            side,
            pl.BlockSpec((depth, width, cells), lambda i: (i, 0, 0)),
        ],
        out_specs=tuple(out_specs),
        compiler_params=pltpu.CompilerParams(vmem_limit_bytes=VMEM_GRANT),
        cost_estimate=pl.CostEstimate(
            flops=fluid.size * 30, bytes_accessed=10 * 2**20, transcendentals=0
        ),
        name="fluid_first" if edges else "fluid_second",
    )(fluid, fluid, fluid, *halos, source)


def exchange(fluid, first_col, last_col):
    streams, azims = lax.axis_size("stream"), lax.axis_size("azim")
    length = fluid.shape[1]
    up = [(i, i + 1) for i in range(streams - 1)]
    down = [(i + 1, i) for i in range(streams - 1)]
    right = [(i, (i + 1) % azims) for i in range(azims)]
    left = [((i + 1) % azims, i) for i in range(azims)]
    sends = (
        (fluid[:, length - 1 :], "stream", up),
        (fluid[:, :1], "stream", down),
        (last_col, "azim", right),
        (first_col, "azim", left),
    )
    halos = []
    for cells, axis, pairs in sends:
        halos.append(lax.ppermute(cells, axis, pairs))
    return tuple(halos)


def on_device(fluid, bubbles, counts, outgoing_block_order, tiles_first_update, tiles_after):
    comps, length, width, cells = fluid.shape
    slots, states, lanes = bubbles.shape
    devices = lax.axis_size("stream") * lax.axis_size("azim")
    cap = slots // devices
    flat = (comps, length * width, cells)
    grid = (length, width, cells)
    axes = ("stream", "azim")
    bubbles = bubbles.transpose(1, 0, 2).reshape(states * slots, lanes)
    halos = exchange(fluid, fluid[:, :, 0], fluid[:, :, width - 1])
    state, amounts = sample_and_advance(
        fluid.reshape(flat), outgoing_block_order, tiles_first_update, counts, bubbles
    )
    sent = state
    if cap % GROUP:
        sent = sent.reshape(slots // GROUP, states, GROUP, lanes).transpose(0, 2, 1, 3)
    arrived = lax.all_to_all(
        sent.reshape(devices, cap * states, lanes), axes,
        split_axis=0, concat_axis=0, tiled=True,
    )
    if cap % GROUP:
        arrived = arrived.reshape(slots // GROUP, GROUP, states, lanes).transpose(0, 2, 1, 3)
    arrived = arrived.reshape(slots // GROUP, states, GROUP, lanes)
    live = (arrived[:, 0, :, 0] * arrived[:, 4, :, 0] >= 0.0).astype(jnp.int32).reshape(slots)
    source = spread_first(
        length * width, cells, outgoing_block_order, tiles_first_update, state, amounts
    )
    fluid, first_col, last_col = fluid_step(True, fluid, halos, source.reshape(grid))
    halos = exchange(fluid, first_col, last_col)
    bubbles, source, void = bubbles_second(
        fluid.reshape(flat), live, tiles_after, arrived.reshape(slots * states, lanes)
    )
    (fluid,) = fluid_step(False, fluid, halos, source.reshape(grid))
    bubbles = bubbles.reshape(states, slots, lanes).transpose(1, 0, 2)
    return fluid, bubbles, void.reshape(grid)


def solution(mesh):
    return jax.shard_map(
        on_device,
        mesh=mesh,
        in_specs=(
            P(None, "stream", "azim", None),
            P(("stream", "azim"), None, None),
            P(("stream", "azim")),
            P(("stream", "azim")),
            P(("stream", "azim")),
            P(("stream", "azim")),
        ),
        out_specs=(
            P(None, "stream", "azim", None),
            P(("stream", "azim"), None, None),
            P("stream", "azim", None),
        ),
        check_vma=False,
    )
```
